32 devices in a mesh: dp: 8 (over y, x, core), head: 4 (over z).
Axes of the slice: x: 2, y: 2, z: 4, core: 2. Of those that a mesh axis runs over, the one named last changes fastest.
Arguments:
- tokens: bfloat16 [2048, 2048], P('dp'), may hold values from -6 to 6
- weights: bfloat16 [4, 768, 2048], P('head', 'dp'), may hold values from -0.13479223 to 0.13479223, as said below
- query_gain: float32 [128], replicated, may hold values from 0.25 to 1.75
- key_gain: float32 [128], replicated, may hold values from 0.25 to 1.75
- first_row: int32 [2048], P('dp'), may hold values from 0 to 2047, as said below
- cotangent: bfloat16 [2048, 2048], P('dp', 'head'), may hold values from -6 to 6
Outputs:
- attended: bfloat16 [2048, 2048], P('dp', 'head')
- token_grad: bfloat16 [2048, 2048], P('dp', 'head')
- weight_grad: float32 [4, 768, 2048], P('head', 'dp')
The draws below stay inside these ranges and needn't reach their ends.
Inputs may be any that keep to these rules, and one draw needn't show every extreme that they name: first_row[i] is the position of the first row of row i's document: documents are runs of consecutive rows, each at most 512 rows long, one of exactly 512 rows, and the last row begins a document of its own. For every even g, weights[g] and weights[g + 1] are equal in their last 256 rows: each key-value head is held by two head devices.
All inputs are finite; a program needn't handle non-finite values.
Results may differ from the reference program's by a relative error of at most 0.017.
Values may be sent and summed in bfloat16 or wider, within the bound.
No kernel may reach another device: no remote copies, remote signals or barrier semaphores. Data moves between devices by JAX's collectives and lax.ppermute only.
A program may use at most 64 MiB of HBM per device.

```python
import math
import jax
import jax.numpy as jnp
from jax import lax

D = 2048
HD = 128
QH_DEV = 4
QHEADS = 16
COLS = 768
ROWS = 256
SPAN = 2
MOST = 512
TOKENS = 2048
N_HEAD = 4


def draw_weights(key, part):
    base = jax.random.normal(jax.random.fold_in(key, 11), (N_HEAD, COLS, D), jnp.float32)
    base = jnp.clip(base, -6.0, 6.0) * (1.0 / D ** 0.5)
    split_row = QH_DEV * HD
    shared = jnp.repeat(base[0::2, split_row:], 2, axis=0)
    return jnp.concatenate([base[:, :split_row], shared], axis=1).astype(jnp.bfloat16)


def draw_first_row(key, part):
    total_rows = TOKENS
    blocks = total_rows // ROWS
    key_period, key_marks, key_place = jax.random.split(jax.random.fold_in(key, 7), 3)
    period = jax.random.randint(key_period, (blocks,), 4, 2 * MOST + 1)
    period_rows = jnp.repeat(period, ROWS)
    random_marks = jax.random.randint(key_marks, (total_rows,), 0, 1048576)
    boundary = random_marks % period_rows == 0
    place_start = jax.random.randint(key_place, (), 0, total_rows - MOST)
    position = jnp.arange(total_rows, dtype=jnp.int32)
    inside = (position > place_start) & (position < place_start + MOST)
    boundary = jnp.where(inside, False, boundary)
    boundary = boundary | (position == place_start) | (position == place_start + MOST) | (position == 0) | (position == total_rows - 1)

    def advance(current, item):
        row_index, row_mark = item
        fresh = row_mark | (row_index - current >= MOST)
        current = jnp.where(fresh, row_index, current)
        return (current, current)
    last_start, starts = lax.scan(advance, jnp.int32(0), (position, boundary))
    return starts.astype(jnp.int32)


def level_of(key, dims, cuts, smallest, largest):
    level = 1.0
    for dim, shards_of in cuts:
        draws = jax.random.uniform(jax.random.fold_in(jax.random.fold_in(key, 6), dim), (shards_of,), jnp.float32, smallest / len(cuts), largest / len(cuts))
        level = level * jnp.repeat(jnp.exp(draws), dims[dim] // shards_of).reshape((-1,) + (1,) * (len(dims) - 1 - dim))
    return level


def normal_values(key, dims, spread, reach, cuts=(), kind=jnp.bfloat16):
    drawn = spread * jax.random.normal(key, dims, jnp.float32)
    if cuts:
        drawn = drawn * level_of(key, dims, cuts, -0.22, 0.18)
    return jnp.clip(drawn, -reach, reach).astype(kind)


def setup_inputs(seed: int = 0) -> dict:
    seeds = jax.random.split(jax.random.key(seed), 7)
    tokens = normal_values(seeds[0], (TOKENS, D), 1.0, 6.0, ((0, 8),))
    weights = draw_weights(jax.random.fold_in(seeds[6], 71), 0)
    query_gain = jnp.clip(1.0 + 0.15 * jax.random.normal(seeds[2], (HD,), jnp.float32), 0.25, 1.75)
    key_gain = jnp.clip(1.0 + 0.15 * jax.random.normal(seeds[3], (HD,), jnp.float32), 0.25, 1.75)
    first_row = draw_first_row(jax.random.fold_in(seeds[6], 71), 0)
    cotangent = normal_values(seeds[5], (TOKENS, QHEADS * HD), 1.0, 6.0, ((0, 8), (1, 4)))
    return {"tokens": tokens, "weights": weights, "query_gain": query_gain, "key_gain": key_gain, "first_row": first_row, "cotangent": cotangent}


EPSILON = 1e-06
THETA = 1000000.0
STRETCH = 0.25

def rounded(values):
    return lax.optimization_barrier(values.astype(jnp.bfloat16)).astype(jnp.float32)

def rope_tables(position, head_size):
    middle = head_size // 2
    channel = jnp.arange(middle, dtype=jnp.float32)
    frequency = THETA ** (-2.0 * channel / head_size)
    angles = (position.astype(jnp.float32) * STRETCH)[:, None] * frequency[None, :]
    angles = jnp.concatenate([angles, angles], axis=1)
    return (jnp.cos(angles), jnp.sin(angles))

def normalize_rotate(values, scaling, cosine_table, sine_table):
    factor = lax.rsqrt(lax.optimization_barrier(jnp.mean(values * values, axis=-1, keepdims=True)) + EPSILON)
    normed = values * factor * scaling
    middle = normed.shape[-1] // 2
    turned = jnp.concatenate([-normed[..., middle:], normed[..., :middle]], axis=-1)
    return normed * cosine_table + turned * sine_table

def prepare(projected, query_gain, key_gain, cosine_table, sine_table):
    head_size = query_gain.shape[0]
    head_count = projected.shape[1] // head_size - 2
    row_count = projected.shape[0]
    queries = projected[:, :head_count * head_size].reshape(row_count, head_count, head_size)
    queries = normalize_rotate(queries, query_gain, cosine_table[:, None, :], sine_table[:, None, :])
    key_part = normalize_rotate(projected[:, head_count * head_size:(head_count + 1) * head_size], key_gain, cosine_table, sine_table)
    value_part = projected[:, (head_count + 1) * head_size:]
    return (queries, key_part, value_part)

def attend_block(queries, key_window, value_window, upstream, first_rows, query_place, key_place):
    head_size = queries.shape[-1]
    score_scale = 1.0 / math.sqrt(head_size)
    visible = (key_place[None, :] >= first_rows[:, None]) & (key_place[None, :] <= query_place[:, None])
    score = jnp.einsum('rhc,kc->rhk', queries.astype(jnp.float32), key_window.astype(jnp.float32)) * score_scale
    weight = jnp.where(visible[:, None, :], jnp.exp(score), 0.0)
    denominator = lax.optimization_barrier(jnp.sum(weight, axis=-1))
    summed = jnp.einsum('rhk,kc->rhc', rounded(weight), value_window.astype(jnp.float32))
    attended = (summed / denominator[..., None]).astype(jnp.bfloat16)
    probability = weight / denominator[..., None]
    upstream_float = upstream.astype(jnp.float32)
    row_delta = lax.optimization_barrier(jnp.sum(upstream_float * attended.astype(jnp.float32), axis=-1))
    grad_prob = jnp.einsum('rhc,kc->rhk', upstream_float, value_window.astype(jnp.float32))
    grad_score = rounded(probability * (grad_prob - row_delta[..., None]) * score_scale)
    grad_query = jnp.einsum('rhk,kc->rhc', grad_score, key_window.astype(jnp.float32))
    grad_key = jnp.einsum('rhk,rhc->kc', grad_score, queries.astype(jnp.float32))
    grad_value = jnp.einsum('rhk,rhc->kc', rounded(probability), upstream_float)
    return (attended, grad_query, grad_key, grad_value)

def reference(tokens, weights, query_gain, key_gain, first_row, cotangent):
    total_rows = tokens.shape[0]
    groups = weights.shape[0]
    head_size = query_gain.shape[0]
    head_count = weights.shape[1] // head_size - 2
    blocks = total_rows // ROWS
    reach_rows = SPAN * ROWS
    window = (SPAN + 1) * ROWS
    position = jnp.arange(total_rows, dtype=jnp.int32)
    cosine_table, sine_table = rope_tables(position, head_size)
    padded_place = jnp.arange(total_rows + reach_rows, dtype=jnp.int32) - reach_rows
    outputs = []
    weight_grads = []
    token_grad = jnp.zeros((total_rows, tokens.shape[1]), jnp.float32)
    for group_index in range(groups):
        projected = jnp.dot(tokens, weights[group_index].T, preferred_element_type=jnp.float32)
        prepared, pullback = jax.vjp(lambda values: prepare(values, query_gain, key_gain, cosine_table, sine_table), projected)
        queries = prepared[0].astype(jnp.bfloat16)
        key_value = jnp.concatenate([prepared[1], prepared[2]], axis=1).astype(jnp.bfloat16)
        padded = jnp.concatenate([jnp.zeros((reach_rows, 2 * head_size), jnp.bfloat16), key_value], axis=0)
        width_begin = group_index * head_count * head_size
        upstream = cotangent[:, width_begin:width_begin + head_count * head_size].reshape(total_rows, head_count, head_size)

        def one_block(block_index):
            block_begin = (block_index * ROWS).astype(jnp.int32)
            block_query = lax.dynamic_slice_in_dim(queries, block_begin, ROWS, 0)
            block_pairs = lax.dynamic_slice_in_dim(padded, block_begin, window, 0)
            block_keys = lax.dynamic_slice_in_dim(padded_place, block_begin, window, 0)
            block_upstream = lax.dynamic_slice_in_dim(upstream, block_begin, ROWS, 0)
            block_first = lax.dynamic_slice_in_dim(first_row, block_begin, ROWS, 0)
            block_rows = lax.dynamic_slice_in_dim(position, block_begin, ROWS, 0)
            return attend_block(block_query, block_pairs[:, :head_size], block_pairs[:, head_size:], block_upstream, block_first, block_rows, block_keys)
        attended, grad_query, grad_key, grad_value = lax.map(one_block, jnp.arange(blocks, dtype=jnp.int32))
        slot_grads = jnp.concatenate([grad_key, grad_value], axis=-1).reshape(blocks, SPAN + 1, ROWS, 2 * head_size)
        collected = jnp.zeros((blocks + SPAN, ROWS, 2 * head_size), jnp.float32)
        for offset in range(SPAN + 1):
            collected = collected + jnp.pad(slot_grads[:, offset], ((offset, SPAN - offset), (0, 0), (0, 0)))
        pair_grad = collected[SPAN:].reshape(total_rows, 2 * head_size)
        grad_projected = pullback((grad_query.reshape(total_rows, head_count, head_size), pair_grad[:, :head_size], pair_grad[:, head_size:]))[0]
        grad_projected = grad_projected.astype(jnp.bfloat16)
        token_grad = token_grad + rounded(jnp.dot(grad_projected, weights[group_index], preferred_element_type=jnp.float32))
        weight_grads.append(jnp.dot(grad_projected.T, tokens, preferred_element_type=jnp.float32))
        outputs.append(attended.reshape(total_rows, head_count * head_size))
    stacked = jnp.stack(weight_grads)
    split_row = head_count * head_size
    partner = stacked.reshape(groups // 2, 2, stacked.shape[1], stacked.shape[2])[:, ::-1].reshape(stacked.shape)
    shared_sum = stacked[:, split_row:] + partner[:, split_row:]
    weight_grad = jnp.concatenate([stacked[:, :split_row], shared_sum], axis=1)
    return (jnp.concatenate(outputs, axis=1), token_grad.astype(jnp.bfloat16), weight_grad)
```

```python
import math

import jax
import jax.numpy as jnp
from jax import lax
from jax.sharding import PartitionSpec as P

MOST = 512
EPSILON = 1e-06
THETA = 1000000.0
STRETCH = 0.25


def swap(x, axis, bits):
    return lax.ppermute(x, axis, [(i, i ^ bits) for i in range(lax.axis_size(axis))])


def rotate(x, axis, by):
    n = lax.axis_size(axis)
    return lax.ppermute(x, axis, [(i, (i + by) % n) for i in range(n)])


def from_behind(x, axis, by):
    devices = lax.axis_size(axis)
    pairs = [(i, i + by) for i in range(devices) if 0 <= i + by < devices]
    return lax.ppermute(x, axis, pairs)


def rope_tables(position, head_size):
    middle = head_size // 2
    channel = jnp.arange(middle, dtype=jnp.float32)
    frequency = THETA ** (-2.0 * channel / head_size)
    angles = (position.astype(jnp.float32) * STRETCH)[:, None] * frequency[None, :]
    angles = jnp.concatenate([angles, angles], axis=1)
    return (jnp.cos(angles), jnp.sin(angles))


def normalize_rotate(values, scaling, cosine_table, sine_table):
    factor = lax.rsqrt(jnp.mean(values * values, axis=-1, keepdims=True) + EPSILON)
    normed = values * factor * scaling
    middle = normed.shape[-1] // 2
    turned = jnp.concatenate([-normed[..., middle:], normed[..., :middle]], axis=-1)
    return normed * cosine_table + turned * sine_table


def prepare(projected, query_gain, key_gain, cosine_table, sine_table):
    hd = query_gain.shape[0]
    heads = projected.shape[1] // hd - 2
    row_count = projected.shape[0]
    queries = projected[:, : heads * hd].reshape(row_count, heads, hd)
    queries = normalize_rotate(
        queries, query_gain, cosine_table[:, None, :], sine_table[:, None, :]
    )
    key_part = normalize_rotate(
        projected[:, heads * hd : (heads + 1) * hd], key_gain, cosine_table, sine_table
    )
    value_part = projected[:, (heads + 1) * hd :]
    return (queries, key_part, value_part)


def attend_window(queries, window, upstream, first_rows, query_place, key_place):
    hd = queries.shape[-1]
    score_scale = 1.0 / math.sqrt(hd)
    key_window = window[:, :hd]
    value_window = window[:, hd:]
    visible = (key_place[None, :] >= first_rows[:, None]) & (
        key_place[None, :] <= query_place[:, None]
    )
    score = (
        jnp.einsum("rhc,kc->rhk", queries, key_window, preferred_element_type=jnp.float32)
        * score_scale
    )
    weight = jnp.where(visible[:, None, :], jnp.exp(score), 0.0)
    denominator = jnp.sum(weight, axis=-1)
    summed = jnp.einsum(
        "rhk,kc->rhc", weight.astype(jnp.bfloat16), value_window, preferred_element_type=jnp.float32
    )
    attended = (summed / denominator[..., None]).astype(jnp.bfloat16)
    probability = weight / denominator[..., None]
    row_delta = jnp.sum(upstream.astype(jnp.float32) * attended.astype(jnp.float32), axis=-1)
    grad_prob = jnp.einsum(
        "rhc,kc->rhk", upstream, value_window, preferred_element_type=jnp.float32
    )
    grad_score = (probability * (grad_prob - row_delta[..., None]) * score_scale).astype(
        jnp.bfloat16
    )
    grad_query = jnp.einsum(
        "rhk,kc->rhc", grad_score, key_window, preferred_element_type=jnp.float32
    )
    grad_key = jnp.einsum("rhk,rhc->kc", grad_score, queries, preferred_element_type=jnp.float32)
    grad_value = jnp.einsum(
        "rhk,rhc->kc",
        probability.astype(jnp.bfloat16),
        upstream,
        preferred_element_type=jnp.float32,
    )
    return (attended, grad_query, jnp.concatenate([grad_key, grad_value], axis=1))


def gather_weights(shard, me):
    n = lax.axis_size("dp")
    if n != 1 << (n.bit_length() - 1) or n > 8:
        return lax.all_gather(shard, "dp", axis=0, tiled=True)
    pieces = {0: shard}
    for bits in sorted(range(2, n, 2), key=lambda b: -bin(b).count("1")):
        pieces[bits] = swap(shard, "dp", bits)
    if n > 1:
        for bits in range(0, n, 2):
            pieces[bits | 1] = swap(pieces[bits], "dp", 1)
    rows = shard.shape[0]
    whole = jnp.zeros((n * rows, shard.shape[1]), shard.dtype)
    for bits in range(n):
        whole = lax.dynamic_update_slice(whole, pieces[bits], ((me ^ bits) * rows, 0))
    return whole


def scatter_weight_grad(grad_t, tokens, other_tokens, me):
    n = lax.axis_size("dp")
    rows = grad_t.shape[0] // n
    product = lambda a, b: jnp.dot(a, b, preferred_element_type=jnp.float32)
    if n != 1 << (n.bit_length() - 1) or n > 8 or n < 2:
        return lax.psum_scatter(product(grad_t, tokens), "dp", scatter_dimension=0, tiled=True)
    piece = lambda bits: lax.dynamic_slice(
        grad_t, ((me ^ bits) * rows, 0), (rows, grad_t.shape[1])
    )
    order = sorted(range(0, n, 2), key=lambda b: -bin(b).count("1"))
    theirs = swap(jnp.concatenate([piece(b | 1) for b in order], axis=0), "dp", 1)
    total = None
    arrived = []
    for at, bits in enumerate(order):
        part = product(piece(bits), tokens) + product(
            theirs[at * rows : (at + 1) * rows], other_tokens
        )
        if bits:
            arrived.append(swap(part.astype(jnp.bfloat16), "dp", bits))
        else:
            total = part
    for part in arrived:
        total = total + part.astype(jnp.float32)
    return total


def body(tokens, weights, query_gain, key_gain, first_row, cotangent):
    hd = query_gain.shape[0]
    rows = tokens.shape[0]
    cols = weights.shape[1] * lax.axis_size("dp")
    heads = cols // hd - 2
    span = -(-MOST // rows)
    me = lax.axis_index("dp")
    position = me * rows + jnp.arange(rows, dtype=jnp.int32)
    key_place = (me - span) * rows + jnp.arange((span + 1) * rows, dtype=jnp.int32)
    cosine_table, sine_table = rope_tables(position, hd)
    weight = gather_weights(weights[0], me)
    other_tokens = swap(tokens, "dp", 1)
    projected = jnp.einsum("rd,cd->rc", tokens, weight, preferred_element_type=jnp.float32)
    prepared, pullback = jax.vjp(
        lambda values: prepare(values, query_gain, key_gain, cosine_table, sine_table), projected
    )
    queries = prepared[0].astype(jnp.bfloat16)
    key_value = jnp.concatenate([prepared[1], prepared[2]], axis=1).astype(jnp.bfloat16)
    earlier = [from_behind(key_value, "dp", distance) for distance in range(span, 0, -1)]
    window = jnp.concatenate(earlier + [key_value], axis=0)
    upstream = cotangent.reshape(rows, heads, hd)
    attended, grad_query, slot_grads = attend_window(
        queries, window, upstream, first_row, position, key_place
    )
    pair_grad = slot_grads[span * rows :]
    for distance in range(1, span + 1):
        slot_index = span - distance
        pair_grad = pair_grad + from_behind(
            slot_grads[slot_index * rows : (slot_index + 1) * rows].astype(jnp.bfloat16),
            "dp",
            -distance,
        ).astype(jnp.float32)
    grad_projected = pullback((grad_query, pair_grad[:, :hd], pair_grad[:, hd:]))[0].astype(
        jnp.bfloat16
    )
    grad_t = grad_projected.T
    shared = swap(grad_t[heads * hd :], "head", 1)
    both = (grad_t[heads * hd :].astype(jnp.float32) + shared.astype(jnp.float32)).astype(
        jnp.bfloat16
    )
    summed_t = jnp.concatenate([grad_t[: heads * hd], both], axis=0)
    partial_grad = jnp.dot(grad_projected, weight, preferred_element_type=jnp.float32).astype(
        jnp.bfloat16
    )
    n_head = lax.axis_size("head")
    g = lax.axis_index("head")
    width = partial_grad.shape[1] // n_head
    chunk = lambda at: lax.dynamic_slice(partial_grad, (0, at * width), (rows, width))
    token_grad = chunk(g).astype(jnp.float32)
    arrived = []
    for by in range(1, n_head):
        arrived.append(rotate(chunk(lax.rem(g + by, n_head)), "head", by))
    weight_grad = scatter_weight_grad(summed_t, tokens, other_tokens, me)
    for part in arrived:
        token_grad = token_grad + part.astype(jnp.float32)
    return (
        attended.reshape(rows, heads * hd),
        token_grad.astype(jnp.bfloat16),
        weight_grad[None],
    )


def solution(mesh):
    in_specs = (P("dp", None), P("head", "dp", None), P(), P(), P("dp"), P("dp", "head"))
    out_specs = (P("dp", "head"), P("dp", "head"), P("head", "dp", None))
    return jax.shard_map(body, mesh=mesh, in_specs=in_specs, out_specs=out_specs, check_vma=False)
```

```python
import math

import jax
import jax.numpy as jnp
from jax import lax
from jax.experimental import pallas as pl
from jax.experimental.pallas import tpu as pltpu
from jax.sharding import PartitionSpec as P


MOST = 512
EPSILON = 1e-06
THETA = 1000000.0
STRETCH = 0.25
BF = jnp.bfloat16
F32 = jnp.float32


def swap(x, axis, bits):
    return lax.ppermute(x, axis, [(i, i ^ bits) for i in range(lax.axis_size(axis))])


def rotate(x, axis, by):
    n = lax.axis_size(axis)
    return lax.ppermute(x, axis, [(i, (i + by) % n) for i in range(n)])


def from_behind(x, axis, by):
    n = lax.axis_size(axis)
    return lax.ppermute(x, axis, [(i, i + by) for i in range(n) if 0 <= i + by < n])


def on_core(kernel, outs, args, flops, scratch=(), after=(), mib=16):
    spec = pl.BlockSpec(memory_space=pltpu.VMEM)
    specs = [
        pl.BlockSpec(memory_space=pltpu.SMEM) if a.ndim == 1 else spec for a in args
    ]
    specs += [pl.BlockSpec(memory_space=pl.ANY)] * len(after)

    def run(*refs):
        kernel(*refs[: len(args)], *refs[len(specs) :])

    return pl.pallas_call(
        run,
        out_shape=[jax.ShapeDtypeStruct(s, d) for s, d in outs],
        in_specs=specs,
        out_specs=[spec] * len(outs),
        scratch_shapes=list(scratch),
        compiler_params=pltpu.CompilerParams(vmem_limit_bytes=mib << 20),
        cost_estimate=pl.CostEstimate(flops=flops, bytes_accessed=1 << 20, transcendentals=0),
    )(*args, *after)


def later(x, after):
    return lax.optimization_barrier((x, after))[0]


def mm(a, b):
    return jnp.dot(a, b, preferred_element_type=F32)


def mm_nt(a, b):
    return lax.dot_general(a, b, (((1,), (1,)), ((), ())), preferred_element_type=F32)


def mm_tn(a, b):
    return lax.dot_general(a, b, (((0,), (0,)), ((), ())), preferred_element_type=F32)


def norm_factor(u):
    return lax.rsqrt(jnp.mean(u * u, axis=0, keepdims=True) + EPSILON)


def rotate_forward(u, gain, cos, sin):
    n = u * norm_factor(u) * gain
    half = n.shape[0] // 2
    a, b = n[:half], n[half:]
    return jnp.concatenate([a * cos - b * sin, b * cos + a * sin], axis=0)


def rotate_backward(grad, u, gain, cos, sin):
    half = u.shape[0] // 2
    a, b = grad[:half], grad[half:]
    inner = jnp.concatenate([a * cos + b * sin, b * cos - a * sin], axis=0) * gain
    factor = norm_factor(u)
    along = jnp.mean(inner * u, axis=0, keepdims=True)
    return factor * (inner - u * (factor * factor * along))


def visible_weights(score, place, first, rows_at, scale):
    rows = first.shape[1]
    keys = score.shape[0]
    key = place + lax.broadcasted_iota(jnp.int32, (keys, rows), 0)
    row = rows_at + lax.broadcasted_iota(jnp.int32, (keys, rows), 1)
    seen = (key >= first) & (key <= row)
    heads = score.shape[1] // rows
    return jnp.concatenate(
        [
            jnp.where(seen, jnp.exp(score[:, h * rows : (h + 1) * rows] * scale), 0.0)
            for h in range(heads)
        ],
        axis=1,
    )


def keys_kernel(me_ref, *refs, count):
    pieces, (gain_ref, cos_ref, sin_ref, proj_ref, kv_ref) = refs[:count], refs[count:]
    rows = pieces[0].shape[0]
    for bits in range(count):
        at = pl.multiple_of((me_ref[0] ^ bits) * rows, 8)
        proj_ref[pl.ds(at, rows), :] = pieces[bits][...]
    hd = gain_ref.shape[0]
    low = proj_ref.shape[0] - 2 * hd
    key = rotate_forward(proj_ref[low : low + hd, :], gain_ref[...], cos_ref[...], sin_ref[...])
    kv_ref[:hd, :] = key.astype(BF)
    kv_ref[hd:, :] = proj_ref[low + hd :, :].astype(BF)


def own_kernel(me_ref, proj_ref, kv_ref, gain_ref, cos_ref, sin_ref, first_ref, up_ref,
               q_ref, weight_ref, prob_ref, sum_ref, den_ref):
    hd = gain_ref.shape[0]
    rows = proj_ref.shape[1]
    heads = proj_ref.shape[0] // hd - 2
    scale = 1.0 / math.sqrt(hd)
    for h in range(heads):
        q_ref[:, h * rows : (h + 1) * rows] = rotate_forward(
            proj_ref[h * hd : (h + 1) * hd, :], gain_ref[...], cos_ref[...], sin_ref[...]
        ).astype(BF)
    score = mm_tn(kv_ref[:hd, :], q_ref[...])
    at = me_ref[0] * rows
    weight = visible_weights(score, at, first_ref[...], at, scale)
    weight_ref[...] = weight
    den_ref[...] = jnp.sum(weight, axis=0, keepdims=True)
    sum_ref[...] = mm(kv_ref[hd:, :], weight.astype(BF))
    prob_ref[...] = mm_tn(kv_ref[hd:, :], up_ref[...])


def block_backward(weight, grad_prob, inverse, delta, scale, q, up):
    prob = weight * inverse
    grad_score = (prob * (grad_prob - delta) * scale).astype(BF)
    grad_key = mm_nt(q, grad_score)
    grad_value = mm_nt(up, prob.astype(BF))
    return grad_score, grad_key, grad_value


def far_kernel(me_ref, *refs, span, hd):
    windows = refs[:span]
    first_ref, up_ref, q_ref, sum_ref, den_ref = refs[span : span + 5]
    att_ref, gq_ref, inv_ref, delta_ref = refs[span + 5 : span + 9]
    slots = refs[span + 9 :]
    rows = first_ref.shape[1]
    heads = q_ref.shape[1] // rows
    scale = 1.0 / math.sqrt(hd)
    total, den = sum_ref[...], den_ref[...]
    weights = []
    for distance in range(1, span + 1):
        kv = windows[distance - 1]
        score = mm_tn(kv[:hd, :], q_ref[...])
        weight = visible_weights(
            score, (me_ref[0] - distance) * rows, first_ref[...], me_ref[0] * rows, scale
        )
        den = den + jnp.sum(weight, axis=0, keepdims=True)
        total = total + mm(kv[hd:, :], weight.astype(BF))
        weights.append(weight)
    inverse = 1.0 / den
    attended = (total * inverse).astype(BF).astype(F32)
    delta = jnp.sum(up_ref[...].astype(F32) * attended, axis=0, keepdims=True)
    for h in range(heads):
        att_ref[:, h * hd : (h + 1) * hd] = attended[:, h * rows : (h + 1) * rows].T.astype(BF)
    grad_query = jnp.zeros(gq_ref.shape, F32)
    for distance in range(1, span + 1):
        kv = windows[distance - 1]
        grad_score, grad_key, grad_value = block_backward(
            weights[distance - 1],
            mm_tn(kv[hd:, :], up_ref[...]),
            inverse,
            delta,
            scale,
            q_ref[...],
            up_ref[...],
        )
        grad_query = grad_query + mm(kv[:hd, :], grad_score)
        slots[distance - 1][:hd, :] = grad_key.astype(BF)
        slots[distance - 1][hd:, :] = grad_value.astype(BF)
    gq_ref[...] = grad_query
    inv_ref[...] = inverse
    delta_ref[...] = delta


def near_kernel(proj_ref, kv_ref, gain_ref, cos_ref, sin_ref, up_ref, q_ref, weight_ref, prob_ref,
                gq_ref, inv_ref, delta_ref, out_ref, slot_ref):
    hd = gain_ref.shape[0]
    rows = proj_ref.shape[1]
    heads = proj_ref.shape[0] // hd - 2
    scale = 1.0 / math.sqrt(hd)
    grad_score, grad_key, grad_value = block_backward(
        weight_ref[...], prob_ref[...], inv_ref[...], delta_ref[...], scale, q_ref[...], up_ref[...]
    )
    slot_ref[:hd, :] = grad_key
    slot_ref[hd:, :] = grad_value
    grad_query = gq_ref[...] + mm(kv_ref[:hd, :], grad_score)
    for h in range(heads):
        out_ref[h * hd : (h + 1) * hd, :] = rotate_backward(
            grad_query[:, h * rows : (h + 1) * rows],
            proj_ref[h * hd : (h + 1) * hd, :],
            gain_ref[...],
            cos_ref[...],
            sin_ref[...],
        ).astype(BF)


def pair_kernel(slot_ref, *refs, count):
    arrived = refs[:count]
    proj_ref, gain_ref, cos_ref, sin_ref, out_ref = refs[count:]
    hd = gain_ref.shape[0]
    total = slot_ref[...]
    for part in arrived:
        total = total + part[...].astype(F32)
    low = proj_ref.shape[0] - 2 * hd
    out_ref[:hd, :] = rotate_backward(
        total[:hd], proj_ref[low : low + hd, :], gain_ref[...], cos_ref[...], sin_ref[...]
    ).astype(BF)
    out_ref[hd:, :] = total[hd:].astype(BF)


def by_bits(n):
    return n >= 2 and n & (n - 1) == 0 and n <= 8


def far_first(n):
    return sorted(range(0, n, 2), key=lambda b: -bin(b).count("1"))


def gather_pieces(shard, n):
    if not by_bits(n):
        return [lax.all_gather(shard, "dp", axis=0, tiled=True)]
    pieces = {0: shard}
    for bits in far_first(n)[:-1]:
        pieces[bits] = swap(shard, "dp", bits)
    for bits in range(0, n, 2):
        pieces[bits | 1] = swap(pieces[bits], "dp", 1)
    return [pieces[bits] for bits in range(n)]


def weights_kernel(me_ref, side_ref, *refs, count, heads_rows, groups):
    pieces, (mine_ref, give_ref, whole_ref) = refs[:count], refs[count:]
    rows = pieces[0].shape[0]
    for bits in range(count):
        at = pl.multiple_of((me_ref[0] ^ bits) * rows, rows)
        whole_ref[pl.ds(at, rows), :] = pieces[bits][...]
    width = whole_ref.shape[1] // groups
    half = give_ref.shape[0]
    low = pl.multiple_of(lax.rem(me_ref[1], heads_rows // half) * half, half)
    for k in range(groups // 2):
        mine = pl.multiple_of((2 * k + side_ref[0]) * width, 128)
        give = pl.multiple_of((2 * k + 1 - side_ref[0]) * width, 128)
        to = slice(k * width, (k + 1) * width)
        mine_ref[:, to] = whole_ref[:, pl.ds(mine, width)]
        give_ref[:, to] = whole_ref[pl.ds(low, half), pl.ds(give, width)]


def token_q_kernel(me_ref, own_ref, their_ref, mine_ref, *refs):
    given, out_ref = refs[:-1], refs[-1]
    rows = own_ref.shape[0]
    total = mm_tn(own_ref[...], mine_ref[:rows, :])
    half = given[0].shape[0]
    for at, part in enumerate(given):
        low = pl.multiple_of(lax.rem(me_ref[0] + at, len(given)) * half, half)
        total = total + mm_tn(their_ref[pl.ds(low, half), :], part[...])
    out_ref[...] = total


def token_kv_kernel(pair_ref, so_far_ref, own_ref, their_ref, mine_ref, both_ref, keep_ref, *refs):
    sends, total_ref = refs[:-1], refs[-1]
    both = (own_ref[...].astype(F32) + their_ref[...].astype(F32)).astype(BF)
    both_ref[...] = both
    low = mine_ref.shape[0] - both.shape[0]
    total_ref[...] = so_far_ref[...] + mm_tn(both, mine_ref[low:, :])
    width = keep_ref.shape[1]
    pairs = len(sends) + 1
    chunk = lambda by: total_ref[
        :, pl.ds(pl.multiple_of(lax.rem(pair_ref[0] + by, pairs) * width, 128), width)
    ]
    keep_ref[...] = chunk(0)
    for by in range(1, pairs):
        sends[by - 1][...] = chunk(by).astype(BF)


def parts_kernel(me_ref, own_q, own_kv, other_q, other_kv, tokens_ref, other_ref, *refs, order):
    outs, (rows_ref, all_ref) = refs[:-2], refs[-2:]
    low, width = own_q.shape
    all_ref[:low, :width] = own_q[...]
    all_ref[low:, :width] = own_kv[...]
    all_ref[:low, width:] = other_q[...]
    all_ref[low:, width:] = other_kv[...]
    rows = outs[0].shape[0]
    for at, bits in enumerate(order):
        start = pl.multiple_of((me_ref[0] ^ bits) * rows, 16)
        rows_ref[at * rows : (at + 1) * rows, :] = all_ref[pl.ds(start, rows), :]
    product = mm(rows_ref[:, :width], tokens_ref[...]) + mm(rows_ref[:, width:], other_ref[...])
    for at, out in enumerate(outs):
        out[...] = product[at * rows : (at + 1) * rows].astype(out.dtype)


def step(tokens, weights, query_gain, key_gain, first_row, cotangent):
    hd = query_gain.shape[0]
    rows = tokens.shape[0]
    n = lax.axis_size("dp")
    cols = weights.shape[1] * n
    heads = cols // hd - 2
    span = -(-MOST // rows)
    me = lax.axis_index("dp")
    where = me.astype(jnp.int32).reshape(1)
    lanes = heads * rows
    position = (me * rows + jnp.arange(rows, dtype=jnp.int32)).astype(F32) * STRETCH
    channel = jnp.arange(hd // 2, dtype=F32)
    angles = (THETA ** (-2.0 * channel / hd))[:, None] * position[None, :]
    cos, sin = jnp.cos(angles), jnp.sin(angles)
    q_gain, k_gain = query_gain.reshape(hd, 1), key_gain.reshape(hd, 1)
    first = first_row.reshape(1, rows)
    up = cotangent.reshape(rows, heads, hd).transpose(2, 1, 0).reshape(hd, lanes)

    pieces = gather_pieces(weights[0], n)
    other_tokens = swap(tokens, "dp", 1) if by_bits(n) else None
    parts = [mm_nt(piece, tokens) for piece in pieces]
    if len(parts) == 1:
        where_keys = jnp.zeros((1,), jnp.int32)
    else:
        where_keys = where
    unit = 2 * rows * lanes * hd
    proj, kv = on_core(
        lambda *r: keys_kernel(*r, count=len(parts)),
        [((cols, rows), F32), ((2 * hd, rows), BF)],
        [where_keys, *parts, k_gain, cos, sin],
        unit,
        after=[up, q_gain, first],
    )
    windows = [from_behind(kv, "dp", distance) for distance in range(1, span + 1)]
    q, weight_own, prob_own, sum_own, den_own = on_core(
        own_kernel,
        [((hd, lanes), BF), ((rows, lanes), F32), ((rows, lanes), F32), ((hd, lanes), F32),
         ((1, lanes), F32)],
        [where, proj, kv, q_gain, cos, sin, first, up],
        4 * unit,
    )
    n_head = lax.axis_size("head")
    g = lax.axis_index("head").astype(jnp.int32)
    pairs = n_head // 2
    split = 2 if by_bits(n) else 1
    q_rows = heads * hd
    width = tokens.shape[1] // n_head
    mine, give = on_core(
        lambda *r: weights_kernel(*r, count=len(pieces), heads_rows=q_rows, groups=n_head),
        [((cols, pairs * width), BF), ((q_rows // split, pairs * width), BF)],
        [jnp.concatenate([where_keys, where]), lax.rem(g, 2).reshape(1), *pieces],
        unit,
        [pltpu.VMEM((cols, tokens.shape[1]), BF)],
        after=[kv],
    )
    given = [swap(give, "head", 1)]
    attended, grad_query, inverse, delta, *slots = on_core(
        lambda *r: far_kernel(*r, span=span, hd=hd),
        [((rows, heads * hd), BF), ((hd, lanes), F32), ((1, lanes), F32), ((1, lanes), F32)]
        + [((2 * hd, rows), BF)] * span,
        [where, *windows, first, up, q, sum_own, den_own],
        12 * unit,
        mib=28,
    )
    arrived = [
        from_behind(slot, "dp", -distance) for distance, slot in zip(range(1, span + 1), slots)
    ]
    grad_q, slot_own = on_core(
        near_kernel,
        [((heads * hd, rows), BF), ((2 * hd, rows), F32)],
        [proj, kv, q_gain, cos, sin, up, q, weight_own, prob_own, grad_query, inverse, delta],
        4 * unit,
    )
    (grad_kv,) = on_core(
        lambda *r: pair_kernel(*r, count=span),
        [((2 * hd, rows), BF)],
        [slot_own, *arrived, proj, k_gain, cos, sin],
        unit,
    )
    if split == 2:
        given.append(swap(later(given[0], grad_q), "dp", 1))
    their_q = swap(grad_q, "head", 1)
    their_kv = swap(grad_kv, "head", 1)
    (so_far,) = on_core(
        token_q_kernel,
        [((rows, pairs * width), F32)],
        [where, grad_q, their_q, mine, *given],
        4 * unit,
    )
    both, token_grad, *sends = on_core(
        token_kv_kernel,
        [((2 * hd, rows), BF), ((rows, width), F32)] + [((rows, width), BF)] * (pairs - 1),
        [lax.div(g, 2).reshape(1), so_far, grad_kv, their_kv, mine],
        unit,
        [pltpu.VMEM((rows, pairs * width), F32)],
    )
    summed = [rotate(part, "head", 2 * by) for by, part in enumerate(sends, 1)]
    if by_bits(n):
        other_q = swap(grad_q, "dp", 1)
        other_kv = swap(both, "dp", 1)
        order = far_first(n)
        shard = cols // n
        *going, weight_grad = on_core(
            lambda *r: parts_kernel(*r, order=order),
            [((shard, tokens.shape[1]), F32 if bits == 0 else BF) for bits in order],
            [where, grad_q, both, other_q, other_kv, tokens, other_tokens],
            4 * unit,
            [pltpu.VMEM((len(order) * shard, 2 * rows), BF), pltpu.VMEM((cols, 2 * rows), BF)],
        )
        for bits, part in zip(order, going):
            weight_grad = weight_grad + swap(part, "dp", bits).astype(F32)
    else:
        weight_grad = lax.psum_scatter(
            mm(jnp.concatenate([grad_q, both], axis=0), tokens),
            "dp",
            scatter_dimension=0,
            tiled=True,
        )
    for part in summed:
        token_grad = token_grad + part.astype(F32)
    return (attended, token_grad.astype(BF), weight_grad[None])


def solution(mesh):
    in_specs = (P("dp", None), P("head", "dp", None), P(), P(), P("dp"), P("dp", "head"))
    out_specs = (P("dp", "head"), P("dp", "head"), P("head", "dp", None))
    return jax.shard_map(step, mesh=mesh, in_specs=in_specs, out_specs=out_specs, check_vma=False)
```
